512 devices in a mesh: tile: 32 (over y, z_lo, core), chan: 16 (over x, z_hi).
Axes of the slice: x: 4, y: 4, z: 16 (z_hi: 4, z_lo: 4; z = z_hi * 4 + z_lo), core: 2. Of those that a mesh axis runs over, the one named last changes fastest.
Arguments:
- features: bfloat16 [256, 1536, 128], P('tile', 'chan'), may hold values from -8 to 8
- dw_weight: float32 [1536, 49], P('chan'), may hold values from -2.5 to 2.5
- dw_bias: float32 [1536], P('chan'), may hold values from -3 to 3
- ln_gain: float32 [1536], replicated, may hold values from 0.5 to 1.5
- ln_bias: float32 [1536], replicated, may hold values from -2 to 2
- w_in: bfloat16 [1536, 6144], P('tile', 'chan'), may hold values from -0.15625 to 0.15625
- b_in: float32 [6144], P('chan'), may hold values from -3 to 3
- w_out: bfloat16 [6144, 1536], P('chan', 'tile'), may hold values from -0.15625 to 0.15625
- b_out: float32 [1536], P('chan'), may hold values from -3 to 3
- gamma: float32 [1536], P('chan'), may hold values from 0.5 to 2
Outputs:
- block_out: bfloat16 [256, 1536, 128], P('tile', 'chan')
The draws below stay inside these ranges and needn't reach their ends.
All inputs are finite; a program needn't handle non-finite values.
Results may differ from the reference program's by a relative error of at most 0.015.
Values may be sent and summed in bfloat16 or wider, within the bound.
A program may use at most 64 MiB of HBM per device.

```python
import math
import jax
import jax.numpy as jnp
from jax import lax

CHANNELS = 1536
EXPANDED = 6144
KERNEL = 7
WIDTH_PX = 128
HEIGHT_PX = 256
N_CHAN = 16


def draw_features(key, part):
    key_base, key_scale = jax.random.split(key, 2)
    scale = jnp.exp(jax.random.uniform(key_scale, (HEIGHT_PX, 1, WIDTH_PX), jnp.float32, math.log(0.5), math.log(2.0)))
    values = jnp.clip(jax.random.normal(key_base, (HEIGHT_PX, CHANNELS, WIDTH_PX), jnp.float32), -4.0, 4.0) * scale
    return values.astype(jnp.bfloat16)


def draw_dw_weight(key, part):
    position = jnp.arange(CHANNELS, dtype=jnp.float32)[:, None] / max(CHANNELS - 1, 1)
    shape_taps = (CHANNELS, KERNEL * KERNEL)
    rising = jnp.exp(position * math.log(3.0))
    values = jnp.clip(jax.random.normal(key, shape_taps, jnp.float32), -4.0, 4.0) / 7.0 * rising
    return values.astype(jnp.float32)


def with_spikes(result, rng, source, target, parts, factor):
    owner, partner = [(jnp.arange(result.shape[axis_at]) // (result.shape[axis_at] // parts)).reshape([-1 if axis == axis_at else 1 for axis in range(result.ndim)]) for axis_at in (source, target)]
    chosen = jax.random.permutation(rng, parts)[partner]
    strong = (owner == chosen) | (owner == (partner + parts // 2) % parts)
    return jnp.where(strong, factor * result, result)


def level_of(rng, extent, cuts, smallest, high):
    loudness, own = 1.0, jax.random.fold_in(rng, 6)
    for dim, parts in cuts:
        steps = jnp.exp(jax.random.uniform(jax.random.fold_in(own, dim), (parts,), jnp.float32, smallest / len(cuts), high / len(cuts)))
        loudness = loudness * jnp.repeat(steps, extent[dim] // parts).reshape([-1 if axis == dim else 1 for axis in range(len(extent))])
    return loudness


def normal_values(own_key, extent, scale, limit, cuts=(), held_as=jnp.bfloat16):
    entries = jax.random.normal(own_key, extent, jnp.float32) * scale
    if len(cuts) > 0:
        entries = level_of(own_key, extent, cuts, -0.22, 0.18) * entries
    return jnp.clip(entries, min=-limit, max=limit).astype(held_as)


def bell_draw_with(stream_key, shape, deviation, limit, shards, heavy, kind=jnp.bfloat16):
    result = deviation * jax.random.normal(stream_key, shape, jnp.float32)
    if shards:
        result = result * level_of(stream_key, shape, shards, -0.22, 0.18)
    return jnp.clip(with_spikes(result, jax.random.fold_in(stream_key, 3), *heavy), -limit, limit).astype(kind)


def setup_inputs(seed: int = 0) -> dict:
    streams_of = jax.random.split(jax.random.key(seed), 11)
    features = draw_features(jax.random.fold_in(streams_of[10], 71), 0)
    dw_weight = draw_dw_weight(jax.random.fold_in(streams_of[10], 71), 0)
    dw_bias = normal_values(streams_of[2], (CHANNELS,), 0.5, 3.0, ((0, 16),), jnp.float32)
    ln_gain = jnp.clip(1.0 + 0.1 * jax.random.normal(streams_of[3], (CHANNELS,), jnp.float32), 0.5, 1.5)
    ln_bias = normal_values(streams_of[4], (CHANNELS,), 0.3, 2.0, (), jnp.float32)
    w_in = normal_values(streams_of[5], (CHANNELS, EXPANDED), CHANNELS ** -0.5, 0.15625, ((0, 32), (1, 16)))
    b_in = normal_values(streams_of[6], (EXPANDED,), 0.5, 3.0, ((0, 16),), jnp.float32)
    w_out = bell_draw_with(streams_of[7], (EXPANDED, CHANNELS), EXPANDED ** -0.5, 0.15625, ((0, 16), (1, 32)), (0, 1, 32, 2.75))
    b_out = normal_values(streams_of[8], (CHANNELS,), 0.5, 3.0, ((0, 16),), jnp.float32)
    gamma = jnp.clip(jnp.exp(math.log(2.0) - 1.3862944 * jax.random.uniform(streams_of[9], (CHANNELS,), jnp.float32) ** level_of(streams_of[9], (CHANNELS,), ((0, 16),), -0.2, 0.2)), 0.5, 2.0)
    return {"features": features, "dw_weight": dw_weight, "dw_bias": dw_bias, "ln_gain": ln_gain, "ln_bias": ln_bias, "w_in": w_in, "b_in": b_in, "w_out": w_out, "b_out": b_out, "gamma": gamma}


def reference(features, dw_weight, dw_bias, ln_gain, ln_bias, w_in, b_in, w_out, b_out, gamma):
    feature_float = features.astype(jnp.float32)
    padded = jnp.pad(feature_float, ((3, 3), (0, 0), (3, 3)))
    convolved = jnp.zeros_like(feature_float) + dw_bias[None, :, None]
    for tap_row in range(KERNEL):
        for tap_col in range(KERNEL):
            window = padded[tap_row:tap_row + HEIGHT_PX, :, tap_col:tap_col + WIDTH_PX]
            convolved = convolved + window * dw_weight[:, tap_row * KERNEL + tap_col][None, :, None]
    conv_out = convolved.astype(jnp.bfloat16)
    values = conv_out.astype(jnp.float32)
    average = lax.optimization_barrier(jnp.mean(values, axis=1, keepdims=True))
    centered = values - average
    variance = lax.optimization_barrier(jnp.mean(centered * centered, axis=1, keepdims=True))
    normed = (centered * lax.rsqrt(variance + 1e-06) * ln_gain[None, :, None] + ln_bias[None, :, None]).astype(jnp.bfloat16)
    flat = jnp.transpose(normed, (0, 2, 1)).reshape(HEIGHT_PX * WIDTH_PX, CHANNELS)
    group = EXPANDED // N_CHAN
    w_in_groups = jnp.transpose(w_in.reshape(CHANNELS, N_CHAN, group), (1, 0, 2))
    b_in_groups = b_in.reshape(N_CHAN, group)
    w_out_groups = w_out.reshape(N_CHAN, group, CHANNELS)

    def add_group(running, pieces):
        weight_in, bias_in, weight_out = pieces
        pre_act = jnp.dot(flat, weight_in, preferred_element_type=jnp.float32) + bias_in[None, :]
        hidden = jax.nn.gelu(pre_act, approximate=False).astype(jnp.bfloat16)
        partial_out = jnp.dot(hidden, weight_out, preferred_element_type=jnp.float32).astype(jnp.bfloat16)
        partial_out = lax.optimization_barrier(partial_out)
        return (running + partial_out.astype(jnp.float32), None)
    start_sum = jnp.zeros((HEIGHT_PX * WIDTH_PX, CHANNELS), jnp.float32)
    summed, _ = lax.scan(add_group, start_sum, (w_in_groups, b_in_groups, w_out_groups))
    projected = (summed + b_out[None, :]).reshape(HEIGHT_PX, WIDTH_PX, CHANNELS)
    projected = jnp.transpose(projected, (0, 2, 1))
    return (feature_float + gamma[None, :, None] * projected).astype(jnp.bfloat16)
```

```python
import functools

import jax
import jax.numpy as jnp
from jax import lax
from jax.experimental import pallas as pl
from jax.experimental.pallas import tpu as pltpu
from jax.sharding import PartitionSpec as P

MESH = pl.DeviceIdType.MESH
F32 = jnp.float32
BF16 = jnp.bfloat16

SLAB = 96
COLS = 384
TALL = 48
BIAS, OUT_BIAS, SCALE = 49, 50, 51

ERF_NUM = (
    0.00022905065861350646,
    0.0034082910107109506,
    0.050955695062380861,
    0.18520832239976145,
    1.128379143519084,
)
ERF_DEN = (
    -1.1791602954361697e-7,
    0.000023547966471313185,
    0.0010179625278914885,
    0.014070470171167667,
    0.11098505178285362,
    0.49746925110067538,
    1.0,
)


def poly(x, coefficients):
    total = jnp.full_like(x, coefficients[0])
    for coefficient in coefficients[1:]:
        total = total * x + coefficient
    return total


def gelu(v):
    u = jnp.clip(v * 0.7071067811865476, -3.832506856900711, 3.832506856900711)
    square = u * u
    erf = u * poly(square, ERF_NUM) / poly(square, ERF_DEN)
    return 0.5 * v * (1.0 + erf)


def body(
    f_ref, table_ref, gain_ref, shift_ref, w_in_ref, b_in_ref, w_out_ref, o_ref,
    ext, cv, xg, xt, hid, ob, rb, pz, fin, W, own_b, bb,
    halo_s, halo_r, za_s, za_r, b_s, b_r, xa_s, xa_r, rs_s, rs_r, fin_s, fin_r,
    zs, zr, ys, yf, yb, yq, cs, cr,
):
    t = lax.axis_index("tile")
    k = lax.axis_index("chan")
    x, zh = lax.div(k, 4), lax.rem(k, 4)
    y, zl, c = lax.div(t, 8), lax.rem(lax.div(t, 2), 4), lax.rem(t, 2)
    z = zh * 4 + zl

    def device(xx, yy, zz, cc):
        return {
            "tile": (yy * 4 + lax.rem(zz, 4)) * 2 + cc,
            "chan": xx * 4 + lax.div(zz, 4),
        }

    def ring(value, size):
        return lax.rem(value + size, size)

    def x_at(e):
        return device(ring(x + e, 4), y, z, c)

    def y_at(e):
        return device(x, ring(y + e, 4), z, c)

    def z_at(e):
        return device(x, y, ring(z + e, 16), c)

    def tile_at(e):
        return {"tile": ring(t + e, 32), "chan": k}

    other = device(x, y, z, 1 - c)

    def send(src, dst, send_sem, recv_sem, to):
        pltpu.make_async_remote_copy(
            src_ref=src, dst_ref=dst, send_sem=send_sem, recv_sem=recv_sem,
            device_id=to, device_id_type=MESH,
        ).start()

    def await_bytes(view, sem):
        pltpu.make_async_copy(view, view, sem).wait()

    barrier = pltpu.get_barrier_semaphore()
    partners = [tile_at(1), tile_at(-1), x_at(1), x_at(2), x_at(3), y_at(1), y_at(-1)]
    partners += [z_at(1), z_at(-1), z_at(4), z_at(8), z_at(-4), other]
    for partner in partners:
        pl.semaphore_signal(barrier, inc=1, device_id=partner, device_id_type=MESH)

    def slot(w, yy, zz):
        return W.at[w, lax.div(zz, 4), yy * 4 + lax.rem(zz, 4), c]

    mine = y * 4 + zl
    W[0, zh, mine, c] = w_in_ref[...]
    eye = (
        lax.broadcasted_iota(jnp.int32, (TALL, TALL), 0)
        == lax.broadcasted_iota(jnp.int32, (TALL, TALL), 1)
    )
    W[1, zh, mine, c] = lax.dot_general(
        jnp.where(eye, 1.0, 0.0).astype(BF16), w_out_ref[...],
        (((1,), (1,)), ((), ())), preferred_element_type=F32,
    ).astype(BF16)
    own_b[...] = jnp.broadcast_to(b_in_ref[...], (8, COLS))
    bb[zh] = own_b[...]
    ext[3:11] = f_ref[...]

    pl.semaphore_wait(barrier, len(partners))

    send(f_ref.at[5:8], ext.at[0:3], halo_s.at[0], halo_r.at[0], tile_at(1))
    send(f_ref.at[0:3], ext.at[11:14], halo_s.at[1], halo_r.at[1], tile_at(-1))

    reach = {(0, 1): 8, (0, -1): 7, (1, 1): 7, (1, -1): 8}

    def spread(w, off):
        zz = ring(z + off, 16)
        piece = slot(w, y, zz)
        for way in (1, -1):
            if off * way <= 0 and -off * way < reach[w, way]:
                send(piece, piece, zs.at[w, (1 - way) // 2],
                     zr.at[w, (1 - way) // 2, -off * way], z_at(way))
        onward = 1 - 2 * w
        send(piece, piece, ys.at[w, 0], yf.at[w, off % 16], y_at(onward))
        send(piece, piece, ys.at[w, 1], yb.at[w], y_at(-onward))

    def pass_on(w, off):
        onward = 1 - 2 * w
        piece = slot(w, ring(y - onward, 4), ring(z + off, 16))
        await_bytes(piece, yf.at[w, off % 16])
        send(piece, piece, ys.at[w, 2], yq.at[w], y_at(onward))

    def tick(s):
        for w in (0, 1):
            for way in (1, -1):
                if s <= reach[w, way]:
                    await_bytes(slot(w, y, ring(z - s * way, 16)), zr.at[w, (1 - way) // 2, s - 1])
                    spread(w, -s * way)
        relay(s - 1)

    def relay(s):
        for w in (0, 1):
            for way in (1, -1):
                if s == 0 and way == 1:
                    pass_on(w, 0)
                if s > 0 and s <= reach[w, way]:
                    pass_on(w, -s * way)

    for w in (0, 1):
        spread(w, 0)

    await_bytes(ext.at[0:3], halo_r.at[0])
    await_bytes(ext.at[11:14], halo_r.at[1])

    @pl.when(t == 0)
    def _():
        ext[0:3] = jnp.zeros((3, SLAB, 128), BF16)

    @pl.when(t == 31)
    def _():
        ext[11:14] = jnp.zeros((3, SLAB, 128), BF16)

    lane = lax.broadcasted_iota(jnp.int32, (1, 1, 128), 2)

    def convolve(i, carry):
        first = pl.multiple_of(lax.div(i, 2) * 16, 16)
        top = lax.rem(i, 2) * 4
        rows = ext[pl.ds(top, 10), pl.ds(first, 16), :].astype(F32)
        table = table_ref[pl.ds(first, 16), :]

        def column(j):
            return jnp.broadcast_to(table[:, j : j + 1], (16, 128))[None]

        total = jnp.broadcast_to(column(BIAS), (4, 16, 128))
        for tap_col in range(7):
            part = rows[0:4] * column(tap_col)
            for tap_row in range(1, 7):
                part = part + rows[tap_row : tap_row + 4] * column(tap_row * 7 + tap_col)
            d = tap_col - 3
            if d != 0:
                part = pltpu.roll(part, (-d) % 128, 2)
                inside = lane < 128 - d if d > 0 else lane >= -d
                part = jnp.where(inside, part, 0.0)
            total = total + part
        cv[pl.ds(top, 4), pl.ds(first, 16), :] = total.astype(BF16)
        return carry

    lax.fori_loop(0, 12, convolve, 0)

    def block(kk):
        return xg.at[:, pl.ds(pl.multiple_of(kk * SLAB, SLAB), SLAB), :]

    for r in (2, 1, 3):
        q = ring(zh + r, 4)
        to = device(x, y, q * 4 + zl, c)
        send(cv.at[pl.ds(2 * q, 2)], block(k), za_s.at[r - 1], za_r.at[r - 1], to)
        send(own_b, bb.at[zh], b_s.at[r - 1], b_r.at[r - 1], to)
    xg[:, pl.ds(pl.multiple_of(k * SLAB, SLAB), SLAB), :] = cv[pl.ds(2 * zh, 2)]

    def share(r):
        kk = x * 4 + ring(zh - r, 4)
        for e in (2, 1, 3):
            send(block(kk), block(kk), xa_s.at[e - 1, r], xa_r.at[e - 1, r], x_at(e))

    def arrived(r):
        await_bytes(block(x * 4 + ring(zh - r, 4)), za_r.at[r - 1])
        share(r)

    share(0)
    tick(1)
    tick(2)
    arrived(1)
    arrived(3)
    tick(3)
    arrived(2)
    tick(4)
    tick(5)
    tick(6)
    tick(7)
    tick(8)
    for r in range(4):
        for e in (1, 2, 3):
            await_bytes(block(ring(x - e, 4) * 4 + ring(zh - r, 4)), xa_r.at[e - 1, r])

    def load(j):
        return xg[:, pl.ds(pl.multiple_of(j * SLAB, SLAB), SLAB), :].astype(F32)

    def fold(v):
        return jnp.sum(v.reshape(2, SLAB // 8, 8, 128), axis=1)

    zero = jnp.zeros((2, 8, 128), F32)
    total = lax.fori_loop(0, 16, lambda j, s: s + fold(load(j)), zero)
    mean = jnp.sum(total, axis=1, keepdims=True) / 1536.0

    def squares(j, s):
        centered = load(j) - mean
        return s + fold(centered * centered)

    total = lax.fori_loop(0, 16, squares, zero)
    scale = lax.rsqrt(jnp.sum(total, axis=1, keepdims=True) / 1536.0 + 1e-6)

    def normalize(j, carry):
        at = pl.ds(pl.multiple_of(j * 128, 128), 128)
        for r in range(2):
            v = (xg[r, at, :].astype(F32) - mean[r]) * scale[r]
            v = v.T * gain_ref[:, at] + shift_ref[:, at]
            xt[r * 128 : r * 128 + 128, at] = v.astype(BF16)
        return carry

    lax.fori_loop(0, 12, normalize, 0)
    relay(8)

    def row(w, yy, cc):
        return W.at[w, :, pl.ds(yy * 4, 4), cc]

    def across(w, o):
        view = row(w, ring(y + o, 4), c)
        send(view, view, cs.at[w, o % 4], cr.at[w, o % 4], other)

    def collect(w):
        onward = 1 - 2 * w
        across(w, 0)
        across(w, -onward)
        await_bytes(row(w, ring(y + onward, 4), c), yb.at[w])
        across(w, onward)
        await_bytes(row(w, ring(y + 2, 4), c), yq.at[w])
        across(w, 2)

    def crossed(w, o):
        await_bytes(row(w, ring(y + o, 4), 1 - c), cr.at[w, o % 4])

    collect(0)
    for r in (1, 2, 3):
        await_bytes(bb.at[ring(zh - r, 4)], b_r.at[r - 1])
    for o in (0, -1, 1, 2):
        crossed(0, o)

    def expand(g, carry):
        pre = jnp.dot(xt[...], W[0, g].reshape(1536, COLS), preferred_element_type=F32)
        hid[g] = gelu(pre + bb[g, 0:1, :]).astype(BF16)
        return carry

    lax.fori_loop(0, 4, expand, 0)
    collect(1)

    for o in (0, 1, -1, 2):
        crossed(1, o)
        to_x = ring(y + o, 4)

        def add(g, s):
            weights = W[1, g, pl.ds(to_x * 4, 4)].reshape(COLS, COLS)
            return s + lax.dot_general(
                weights, hid[g], (((1,), (1,)), ((), ())), preferred_element_type=F32
            )

        part = lax.fori_loop(0, 4, add, jnp.zeros((COLS, 256), F32)).astype(BF16)
        ob[to_x, 0] = part[:, 0:128]
        ob[to_x, 1] = part[:, 128:256]

        @pl.when(to_x != x)
        def _():
            send(ob.at[to_x], rb.at[x], rs_s.at[to_x], rs_r.at[x], device(to_x, y, z, c))

    for e in (1, 2, 3):
        await_bytes(rb.at[ring(x + e, 4)], rs_r.at[ring(x + e, 4)])

    def reduce(i, carry):
        at = pl.ds(pl.multiple_of(i * 32, 32), 32)
        s = ob[x, :, at, :].astype(F32)
        for e in (1, 2, 3):
            s = s + rb[ring(x + e, 4), :, at, :].astype(F32)
        pz[:, at, :] = s.astype(BF16)
        return carry

    lax.fori_loop(0, 12, reduce, 0)

    for r in (2, 1, 3):
        q = ring(zh + r, 4)
        to = device(x, y, q * 4 + zl, c)
        src = pz.at[:, pl.ds(pl.multiple_of(q * SLAB, SLAB), SLAB), :]
        send(src, fin.at[pl.ds(2 * zh, 2)], fin_s.at[r - 1], fin_r.at[r - 1], to)
    fin[pl.ds(2 * zh, 2)] = pz[:, pl.ds(pl.multiple_of(zh * SLAB, SLAB), SLAB), :]
    for r in (1, 3, 2):
        await_bytes(fin.at[pl.ds(2 * ring(zh - r, 4), 2)], fin_r.at[r - 1])

    def finish(i, carry):
        at = pl.ds(pl.multiple_of(i * 16, 16), 16)
        table = table_ref[at, :]
        shift = jnp.broadcast_to(table[:, OUT_BIAS : OUT_BIAS + 1], (16, 128))[None]
        gamma = jnp.broadcast_to(table[:, SCALE : SCALE + 1], (16, 128))[None]
        projected = fin[:, at, :].astype(F32) + shift
        o_ref[:, at, :] = (f_ref[:, at, :].astype(F32) + gamma * projected).astype(BF16)
        return carry

    lax.fori_loop(0, 6, finish, 0)

    await_bytes(f_ref.at[5:8], halo_s.at[0])
    await_bytes(f_ref.at[0:3], halo_s.at[1])
    for r in range(3):
        await_bytes(cv.at[0:2], za_s.at[r])
        await_bytes(own_b, b_s.at[r])
        await_bytes(cv.at[0:2], fin_s.at[r])
        for b in range(4):
            await_bytes(cv.at[0:2], xa_s.at[r, b])
        await_bytes(ob.at[0], rs_s.at[ring(x + r + 1, 4)])
    for w in (0, 1):
        for way in (1, -1):
            count = reach[w, way]
            view = W.at[w, 0, 0:count, c]
            await_bytes(view, zs.at[w, (1 - way) // 2])
        for i in range(3):
            await_bytes(row(w, y, c), ys.at[w, i])
        for o in range(4):
            await_bytes(row(w, y, c), cs.at[w, o])


def local(features, dw_weight, dw_bias, ln_gain, ln_bias, w_in, b_in, w_out, b_out, gamma):
    table = jnp.concatenate(
        [dw_weight, dw_bias[:, None], b_out[:, None], gamma[:, None]], axis=1
    )
    dma = pltpu.SemaphoreType.DMA
    vmem = pl.BlockSpec(memory_space=pltpu.VMEM)
    return pl.pallas_call(
        body,
        out_shape=jax.ShapeDtypeStruct(features.shape, BF16),
        in_specs=[vmem] * 7,
        out_specs=vmem,
        scratch_shapes=[
            pltpu.VMEM((14, SLAB, 128), BF16),
            pltpu.VMEM((8, SLAB, 128), BF16),
            pltpu.VMEM((2, 1536, 128), BF16),
            pltpu.VMEM((256, 1536), BF16),
            pltpu.VMEM((4, 256, COLS), BF16),
            pltpu.VMEM((4, 2, COLS, 128), BF16),
            pltpu.VMEM((4, 2, COLS, 128), BF16),
            pltpu.VMEM((2, COLS, 128), BF16),
            pltpu.VMEM((8, SLAB, 128), BF16),
            pltpu.VMEM((2, 4, 16, 2, TALL, COLS), BF16),
            pltpu.VMEM((8, COLS), F32),
            pltpu.VMEM((4, 8, COLS), F32),
            dma((2,)), dma((2,)),
            dma((3,)), dma((3,)),
            dma((3,)), dma((3,)),
            dma((3, 4)), dma((3, 4)),
            dma((4,)), dma((4,)),
            dma((3,)), dma((3,)),
            dma((2, 2)), dma((2, 2, 8)),
            dma((2, 3)), dma((2, 16)), dma((2,)), dma((2,)),
            dma((2, 4)), dma((2, 4)),
        ],
        compiler_params=pltpu.CompilerParams(
            collective_id=0, has_side_effects=True, vmem_limit_bytes=48 * 2**20
        ),
        name="block",
    )(
        features, table, ln_gain[None, :], ln_bias[None, :], w_in, b_in[None, :], w_out
    )


def solution(mesh):
    placed = (
        P("tile", "chan", None),
        P("chan", None),
        P("chan"),
        P(),
        P(),
        P("tile", "chan"),
        P("chan"),
        P("chan", "tile"),
        P("chan"),
        P("chan"),
    )
    return jax.shard_map(
        local, mesh=mesh, in_specs=placed, out_specs=P("tile", "chan", None), check_vma=False
    )
```

```python
import functools

import jax
import jax.numpy as jnp
from jax import lax
from jax.experimental import pallas as pl
from jax.experimental.pallas import tpu as pltpu
from jax.sharding import PartitionSpec as P

MESH = pl.DeviceIdType.MESH
F32 = jnp.float32
BF16 = jnp.bfloat16

SLAB = 96
COLS = 384
TALL = 48
TAPS = 49
FIRST, SECOND = 4, 6
LAG = 0
BIAS, OUT_BIAS, SCALE = 49, 50, 51

ERF_NUM = (
    0.00022905065861350646,
    0.0034082910107109506,
    0.050955695062380861,
    0.18520832239976145,
    1.128379143519084,
)
ERF_DEN = (
    -1.1791602954361697e-7,
    0.000023547966471313185,
    0.0010179625278914885,
    0.014070470171167667,
    0.11098505178285362,
    0.49746925110067538,
    1.0,
)


def poly(x, coefficients):
    total = jnp.full_like(x, coefficients[0])
    for coefficient in coefficients[1:]:
        total = total * x + coefficient
    return total


def gelu(v):
    u = jnp.clip(v * 0.7071067811865476, -3.832506856900711, 3.832506856900711)
    square = u * u
    erf = u * poly(square, ERF_NUM) / poly(square, ERF_DEN)
    return 0.5 * v * (1.0 + erf)


def body(
    f_hbm, table_hbm, dw_bias_hbm, b_out_hbm, gamma_hbm, gain_hbm, shift_hbm, w_in_hbm,
    b_in_hbm, w_out_hbm, o_ref,
    f_ref, table_ref, dw_bias_ref, b_out_ref, gamma_ref, gain_ref, shift_ref, b_in_ref,
    fetch_s, columns, planes, wide, halo, conv, cv, xg, xt, hid, ob, rb, pz, fin, W, own_b, bb,
    halo_s, halo_r, za_s, za_r, b_s, b_r, xa_s, xa_r, rs_s, rs_r, fin_s, fin_r,
    zs, zr, ys, yf, yb, yq, cs, cr,
):
    t = lax.axis_index("tile")
    k = lax.axis_index("chan")
    x, zh = lax.div(k, 4), lax.rem(k, 4)
    y, zl, c = lax.div(t, 8), lax.rem(lax.div(t, 2), 4), lax.rem(t, 2)
    z = zh * 4 + zl

    def device(xx, yy, zz, cc):
        return {
            "tile": (yy * 4 + lax.rem(zz, 4)) * 2 + cc,
            "chan": xx * 4 + lax.div(zz, 4),
        }

    def ring(value, size):
        return lax.rem(value + size, size)

    def x_at(e):
        return device(ring(x + e, 4), y, z, c)

    def y_at(e):
        return device(x, ring(y + e, 4), z, c)

    def z_at(e):
        return device(x, y, ring(z + e, 16), c)

    def tile_at(e):
        return {"tile": ring(t + e, 32), "chan": k}

    other = device(x, y, z, 1 - c)

    def send(src, dst, send_sem, recv_sem, to):
        pltpu.make_async_remote_copy(
            src_ref=src, dst_ref=dst, send_sem=send_sem, recv_sem=recv_sem,
            device_id=to, device_id_type=MESH,
        ).start()

    def await_bytes(view, sem):
        pltpu.make_async_copy(view, view, sem).wait()

    mine = y * 4 + zl
    fetches = [
        pltpu.make_async_copy(src, dst, fetch_s.at[i])
        for i, (src, dst) in enumerate((
            (w_in_hbm, W.at[0, zh, mine, c]), (w_out_hbm, W.at[1, zh, mine, c]), (f_hbm, f_ref),
            (table_hbm, table_ref), (dw_bias_hbm, dw_bias_ref), (b_out_hbm, b_out_ref),
            (gamma_hbm, gamma_ref), (gain_hbm, gain_ref), (shift_hbm, shift_ref),
            (b_in_hbm, b_in_ref),
        ))
    ]

    barrier = pltpu.get_barrier_semaphore()
    partners = [tile_at(1), tile_at(-1), x_at(1), x_at(2), x_at(3), y_at(1), y_at(-1)]
    partners += [z_at(1), z_at(-1), z_at(2), z_at(-2), z_at(6), z_at(-6), other]
    for partner in partners:
        pl.semaphore_signal(barrier, inc=1, device_id=partner, device_id_type=MESH)
    for fetch in fetches:
        fetch.start()

    def slot(w, yy, zz):
        return W.at[w, lax.div(zz, 4), yy * 4 + lax.rem(zz, 4), c]

    for fetch in fetches:
        fetch.wait()
    pl.semaphore_wait(barrier, len(partners))

    send(f_ref.at[5:8], halo.at[0], halo_s.at[0], halo_r.at[0], tile_at(1))
    send(f_ref.at[0:3], halo.at[1], halo_s.at[1], halo_r.at[1], tile_at(-1))

    reach = {(0, 1): 8, (0, -1): 7, (1, 1): 7, (1, -1): 8}

    def spread(w, off):
        zz = ring(z + off, 16)
        piece = slot(w, y, zz)
        for way in (1, -1):
            if off * way <= 0 and -off * way < reach[w, way]:
                send(piece, piece, zs.at[w, (1 - way) // 2],
                     zr.at[w, (1 - way) // 2, -off * way], z_at(way))
        onward = heading(w, off)
        send(piece, piece, ys.at[w, 0], yf.at[w, off % 16], y_at(onward))
        send(piece, piece, ys.at[w, 1], yb.at[w, off % 16], y_at(-onward))
        cross(w, 0, piece)

    def cross(w, o, piece):
        send(piece, piece, cs.at[w, o], cr.at[w, o], other)

    def heading(w, off):
        return 1 if off < 0 or (off == 0 and w == 0) else -1

    def pass_on(w, off):
        onward = heading(w, off)
        piece = slot(w, ring(y - onward, 4), ring(z + off, 16))
        await_bytes(piece, yf.at[w, off % 16])
        send(piece, piece, ys.at[w, 2], yq.at[w, off % 16], y_at(onward))
        cross(w, -onward % 4, piece)
        piece = slot(w, ring(y + onward, 4), ring(z + off, 16))
        await_bytes(piece, yb.at[w, off % 16])
        cross(w, onward % 4, piece)

    def last(w, off):
        piece = slot(w, ring(y + 2, 4), ring(z + off, 16))
        await_bytes(piece, yq.at[w, off % 16])
        cross(w, 2, piece)

    def tick(w, s):
        for way in (1, -1):
            if s <= reach[w, way]:
                await_bytes(slot(w, y, ring(z - s * way, 16)), zr.at[w, (1 - way) // 2, s - 1])
                spread(w, -s * way)

    def relay(w, s, action):
        for way in (1, -1):
            if s == 0 and way == 1:
                action(w, 0)
            if s > 0 and s <= reach[w, way]:
                action(w, -s * way)

    spread(0, 0)
    spread(1, 0)

    for j in range(3):
        own_b[:, 128 * j : 128 * j + 128] = jnp.broadcast_to(b_in_ref[j : j + 1, :], (8, 128))

    def step(s):
        for w, at in ((0, s), (1, s - LAG)):
            if w == 1 and at == 0:
                spread(1, 0)
            if 1 <= at <= 8:
                tick(w, at)
            if 1 <= at <= 9:
                relay(w, at - 1, pass_on)
            if 2 <= at <= 10:
                relay(w, at - 2, last)

    lane = lax.broadcasted_iota(jnp.int32, (1, 128), 1)
    columns[...] = table_ref[...].T

    def spread_table(i, carry):
        at = pl.ds(pl.multiple_of(i * 8, 8), 8)
        table = columns[at, :]
        for j in range(TAPS):
            d = j % 7 - 3
            value = jnp.broadcast_to(table[:, j : j + 1], (8, 128))
            if d != 0:
                inside = lane >= d if d > 0 else lane < 128 + d
                value = jnp.where(inside, value, 0.0)
            planes[j, at, :] = value
        diagonal = (
            lax.broadcasted_iota(jnp.int32, (8, SLAB), 0) + i * 8
            == lax.broadcasted_iota(jnp.int32, (8, SLAB), 1)
        )
        for j, ref in ((BIAS, dw_bias_ref), (OUT_BIAS, b_out_ref), (SCALE, gamma_ref)):
            column = jnp.sum(jnp.where(diagonal, ref[...], 0.0), axis=1, keepdims=True)
            planes[j, at, :] = jnp.broadcast_to(column, (8, 128))
        return carry

    lax.fori_loop(0, 12, spread_table, 0)

    def widen(i, carry):
        at = pl.ds(pl.multiple_of(i * 16, 16), 16)
        wide[:, at, :] = f_ref[:, at, :].astype(F32)
        return carry

    lax.fori_loop(0, 6, widen, 0)

    def taps(rows, at, pairs):
        total = [None] * len(pairs)
        for tap_col in range(7):
            d = tap_col - 3
            weight = {}
            for r, pair in enumerate(pairs):
                part = None
                for e, tap_row in pair:
                    if tap_row not in weight:
                        weight[tap_row] = planes[tap_row * 7 + tap_col, at, :]
                    product = rows[e] * weight[tap_row]
                    part = product if part is None else part + product
                if d != 0:
                    part = pltpu.roll(part, (-d) % 128, 1)
                total[r] = part if total[r] is None else total[r] + part
        return total

    def own_rows(i, carry):
        at = pl.ds(pl.multiple_of(i * 8, 8), 8)
        rows = [wide[r, at, :] for r in range(8)]
        pairs = [[(e, e - r + 3) for e in range(8) if 0 <= e - r + 3 < 7] for r in range(8)]
        bias = planes[BIAS, at, :]
        for r, part in enumerate(taps(rows, at, pairs)):
            conv[r, at, :] = part + bias
        return carry

    lax.fori_loop(0, 12, own_rows, 0)
    step(1)

    await_bytes(halo.at[0], halo_r.at[0])
    await_bytes(halo.at[1], halo_r.at[1])

    @pl.when(t == 0)
    def _():
        halo[0] = jnp.zeros((3, SLAB, 128), BF16)

    @pl.when(t == 31)
    def _():
        halo[1] = jnp.zeros((3, SLAB, 128), BF16)

    def rims(i, carry):
        at = pl.ds(pl.multiple_of(i * 16, 16), 16)
        for side, first in ((0, 0), (1, 5)):
            rows = [halo[side, r, at, :].astype(F32) for r in range(3)]
            if side == 0:
                pairs = [[(e, e - r) for e in range(r, 3)] for r in range(3)]
            else:
                pairs = [[(e, e - r + 6) for e in range(r + 1)] for r in range(3)]
            for r, part in enumerate(taps(rows, at, pairs)):
                cv[first + r, at, :] = (conv[first + r, at, :] + part).astype(BF16)
        for r in (3, 4):
            cv[r, at, :] = conv[r, at, :].astype(BF16)
        return carry

    lax.fori_loop(0, 6, rims, 0)

    def block(kk):
        return xg.at[:, pl.ds(pl.multiple_of(kk * SLAB, SLAB), SLAB), :]

    for r in (1, 2, 0, 3):
        rows = pl.ds(2 * ring(zh + r, 4), 2)
        send(cv.at[rows], block(k), za_s.at[r], za_r.at[r], z_at(2 + 4 * r - 16 * (r // 2)))
    for r in range(4):
        to = z_at(2 + 4 * r - 16 * (r // 2))
        send(own_b, bb.at[zh], b_s.at[r], b_r.at[r], to)

    unit = ring(z - 2, 16)
    place, line = lax.div(unit, 4), lax.rem(unit, 4)

    def source(r):
        return ring(place - r, 4)

    def share(r):
        kk = x * 4 + source(r)
        for e in (2, 1, 3):
            send(block(kk), block(kk), xa_s.at[e - 1, r], xa_r.at[e - 1, r], x_at(e))

    def arrived(r):
        await_bytes(block(x * 4 + source(r)), za_r.at[r])
        share(r)

    for s in range(2, 11):
        step(s)
        if s == FIRST:
            arrived(0)
            arrived(3)
        if s == SECOND:
            arrived(1)
            arrived(2)
    for r in range(4):
        for e in (1, 2, 3):
            await_bytes(block(ring(x - e, 4) * 4 + source(r)), xa_r.at[e - 1, r])

    def load(j):
        return xg[:, pl.ds(pl.multiple_of(j * SLAB, SLAB), SLAB), :].astype(F32)

    def fold(v):
        return jnp.sum(v.reshape(2, SLAB // 8, 8, 128), axis=1)

    zero = jnp.zeros((2, 8, 128), F32)
    total = lax.fori_loop(0, 16, lambda j, s: s + fold(load(j)), zero)
    mean = jnp.sum(total, axis=1, keepdims=True) / 1536.0

    def squares(j, s):
        centered = load(j) - mean
        return s + fold(centered * centered)

    total = lax.fori_loop(0, 16, squares, zero)
    scale = lax.rsqrt(jnp.sum(total, axis=1, keepdims=True) / 1536.0 + 1e-6)

    def normalize(j, carry):
        at = pl.ds(pl.multiple_of(j * 128, 128), 128)
        for r in range(2):
            v = (xg[r, at, :].astype(F32) - mean[r]) * scale[r]
            v = v.T * gain_ref[pl.ds(j, 1), :] + shift_ref[pl.ds(j, 1), :]
            xt[r * 128 : r * 128 + 128, at] = v.astype(BF16)
        return carry

    lax.fori_loop(0, 12, normalize, 0)

    def row(w, yy, cc):
        return W.at[w, :, pl.ds(yy * 4, 4), cc]

    def crossed(w, o):
        await_bytes(row(w, ring(y + o, 4), 1 - c), cr.at[w, o % 4])

    for r in range(4):
        await_bytes(bb.at[source(r)], b_r.at[r])
    for o in (0, -1, 1, 2):
        crossed(0, o)

    for g in range(4):
        pre = jnp.dot(xt[...], W[0, g].reshape(1536, COLS), preferred_element_type=F32)
        hid[g] = gelu(pre + bb[g, 0:1, :]).T.astype(BF16)
        if g + 11 <= LAG + 10:
            step(g + 11)

    def project(o):
        crossed(1, o)
        to_x = ring(y + o, 4)
        for half in range(2):
            part = jnp.zeros((COLS // 2, 256), F32)
            for g in range(4):
                weights = W[1, g, pl.ds(to_x * 4 + 2 * half, 2)].reshape(COLS // 2, COLS)
                part = part + jnp.dot(weights, hid[g], preferred_element_type=F32)
            part = part.astype(BF16)
            at = slice(half * (COLS // 2), (half + 1) * (COLS // 2))
            ob[to_x, 0, at] = part[:, 0:128]
            ob[to_x, 1, at] = part[:, 128:256]

        give(to_x, 0)

    def give(to_x, r):
        @pl.when(to_x != x)
        def _():
            send(
                ob.at[to_x, r], rb.at[x, r], rs_s.at[to_x, r], rs_r.at[x, r],
                device(to_x, y, z, c),
            )

    for o in (0, 1, -1, 2):
        project(o)
    for o in (0, 1, -1, 2):
        give(ring(y + o, 4), 1)

    for r in range(2):
        for e in (1, 2, 3):
            await_bytes(rb.at[ring(x + e, 4), r], rs_r.at[ring(x + e, 4), r])

        def reduce(i, carry):
            at = pl.ds(pl.multiple_of(i * 32, 32), 32)
            s = ob[x, r, at, :].astype(F32)
            for e in (1, 2, 3):
                s = s + rb[ring(x + e, 4), r, at, :].astype(F32)
            pz[r, at, :] = s.astype(BF16)
            return carry

        lax.fori_loop(0, 12, reduce, 0)
        for n in (1, 2, 0, 3):
            home = source(n)
            src = pz.at[r, pl.ds(pl.multiple_of(home * SLAB, SLAB), SLAB), :]
            send(
                src, fin.at[2 * place + r], fin_s.at[n, r], fin_r.at[n, r],
                device(x, y, home * 4 + line, c),
            )
    for r in range(2):
        for n in (0, 3, 1, 2):
            await_bytes(fin.at[2 * ring(zh + n, 4) + r], fin_r.at[n, r])

    def finish(i, carry):
        at = pl.ds(pl.multiple_of(i * 16, 16), 16)
        projected = fin[:, at, :].astype(F32) + planes[OUT_BIAS, at, :]
        o_ref[:, at, :] = (wide[:, at, :] + planes[SCALE, at, :] * projected).astype(BF16)
        return carry

    lax.fori_loop(0, 6, finish, 0)

    await_bytes(f_ref.at[5:8], halo_s.at[0])
    await_bytes(f_ref.at[0:3], halo_s.at[1])
    for n in range(4):
        await_bytes(cv.at[0:2], za_s.at[n])
        await_bytes(own_b, b_s.at[n])
        for e in range(3):
            await_bytes(cv.at[0:2], xa_s.at[e, n])
        for r in range(2):
            await_bytes(cv.at[0], fin_s.at[n, r])
            if n > 0:
                await_bytes(ob.at[0, 0], rs_s.at[ring(x + n, 4), r])
    for w in (0, 1):
        for way in (1, -1):
            count = reach[w, way]
            view = W.at[w, 0, 0:count, c]
            await_bytes(view, zs.at[w, (1 - way) // 2])
        for i in range(3):
            await_bytes(row(w, y, c), ys.at[w, i])
        for o in range(4):
            await_bytes(row(w, y, c), cs.at[w, o])


def local(features, dw_weight, dw_bias, ln_gain, ln_bias, w_in, b_in, w_out, b_out, gamma):
    dma = pltpu.SemaphoreType.DMA
    vmem = pl.BlockSpec(memory_space=pltpu.VMEM)
    return pl.pallas_call(
        body,
        out_shape=jax.ShapeDtypeStruct(features.shape, BF16),
        in_specs=[pl.BlockSpec(memory_space=pltpu.HBM)] * 10,
        out_specs=vmem,
        scratch_shapes=[
            pltpu.VMEM((8, SLAB, 128), BF16),
            pltpu.VMEM((TAPS, SLAB), F32),
            pltpu.VMEM((1, SLAB), F32),
            pltpu.VMEM((1, SLAB), F32),
            pltpu.VMEM((1, SLAB), F32),
            pltpu.VMEM((12, 128), F32),
            pltpu.VMEM((12, 128), F32),
            pltpu.VMEM((3, 128), F32),
            dma((10,)),
            pltpu.VMEM((SLAB, TAPS), F32),
            pltpu.VMEM((TAPS + 3, SLAB, 128), F32),
            pltpu.VMEM((8, SLAB, 128), F32),
            pltpu.VMEM((2, 3, SLAB, 128), BF16),
            pltpu.VMEM((8, SLAB, 128), F32),
            pltpu.VMEM((8, SLAB, 128), BF16),
            pltpu.VMEM((2, 1536, 128), BF16),
            pltpu.VMEM((256, 1536), BF16),
            pltpu.VMEM((4, COLS, 256), BF16),
            pltpu.VMEM((4, 2, COLS, 128), BF16),
            pltpu.VMEM((4, 2, COLS, 128), BF16),
            pltpu.VMEM((2, COLS, 128), BF16),
            pltpu.VMEM((8, SLAB, 128), BF16),
            pltpu.VMEM((2, 4, 16, 2, TALL, COLS), BF16),
            pltpu.VMEM((8, COLS), F32),
            pltpu.VMEM((4, 8, COLS), F32),
            dma((2,)), dma((2,)),
            dma((4,)), dma((4,)),
            dma((4,)), dma((4,)),
            dma((3, 4)), dma((3, 4)),
            dma((4, 2)), dma((4, 2)),
            dma((4, 2)), dma((4, 2)),
            dma((2, 2)), dma((2, 2, 8)),
            dma((2, 3)), dma((2, 16)), dma((2, 16)), dma((2, 16)),
            dma((2, 4)), dma((2, 4)),
        ],
        compiler_params=pltpu.CompilerParams(
            collective_id=0, has_side_effects=True, vmem_limit_bytes=62 * 2**20
        ),
        name="block",
    )(
        features, dw_weight.T, dw_bias[None, :], b_out[None, :], gamma[None, :],
        ln_gain.reshape(12, 128), ln_bias.reshape(12, 128), w_in, b_in.reshape(3, 128), w_out.T,
    )


def solution(mesh):
    placed = (
        P("tile", "chan", None),
        P("chan", None),
        P("chan"),
        P(),
        P(),
        P("tile", "chan"),
        P("chan"),
        P("chan", "tile"),
        P("chan"),
        P("chan"),
    )
    return jax.shard_map(
        local, mesh=mesh, in_specs=placed, out_specs=P("tile", "chan", None), check_vma=False
    )
```

```python
import functools

import jax
import jax.numpy as jnp
from jax import lax
from jax.experimental import pallas as pl
from jax.experimental.pallas import tpu as pltpu
from jax.sharding import PartitionSpec as P

MESH = pl.DeviceIdType.MESH
F32 = jnp.float32
BF16 = jnp.bfloat16

SLAB = 96
COLS = 384
TALL = 48
HEAD = 80
TAPS = 49
FIRST, SECOND = 7, 9
BIAS, OUT_BIAS, SCALE = 49, 50, 51

ERF_NUM = (
    0.00022905065861350646,
    0.0034082910107109506,
    0.050955695062380861,
    0.18520832239976145,
    1.128379143519084,
)
ERF_DEN = (
    -1.1791602954361697e-7,
    0.000023547966471313185,
    0.0010179625278914885,
    0.014070470171167667,
    0.11098505178285362,
    0.49746925110067538,
    1.0,
)


def poly(x, coefficients):
    total = jnp.full_like(x, coefficients[0])
    for coefficient in coefficients[1:]:
        total = total * x + coefficient
    return total


def gelu(v):
    u = jnp.clip(v * 0.7071067811865476, -3.832506856900711, 3.832506856900711)
    square = u * u
    erf = u * poly(square, ERF_NUM) / poly(square, ERF_DEN)
    return 0.5 * v * (1.0 + erf)


def body(
    f_hbm, table_hbm, dw_bias_hbm, b_out_hbm, gamma_hbm, gain_hbm, shift_hbm, w_in_hbm,
    b_in_hbm, w_out_hbm, o_ref,
    f_ref, table_ref, dw_bias_ref, b_out_ref, gamma_ref, gain_ref, shift_ref, b_in_ref,
    fetch_s, columns, planes, wide, halo, conv, cv, xg, xt, hid, ob, rb, pz, fin, W, own_b, bb,
    halo_s, halo_r, za_s, za_r, b_s, b_r, xa_s, xa_r, rs_s, rs_r, fin_s, fin_r,
    zs, zr, ys, yf, yb, yq, cs, cr, ty_s, ty_r, ts, tr, tc_s, tc_r,
):
    t = lax.axis_index("tile")
    k = lax.axis_index("chan")
    x, zh = lax.div(k, 4), lax.rem(k, 4)
    y, zl, c = lax.div(t, 8), lax.rem(lax.div(t, 2), 4), lax.rem(t, 2)
    z = zh * 4 + zl

    def device(xx, yy, zz, cc):
        return {
            "tile": (yy * 4 + lax.rem(zz, 4)) * 2 + cc,
            "chan": xx * 4 + lax.div(zz, 4),
        }

    def ring(value, size):
        return lax.rem(value + size, size)

    def x_at(e):
        return device(ring(x + e, 4), y, z, c)

    def y_at(e):
        return device(x, ring(y + e, 4), z, c)

    def z_at(e):
        return device(x, y, ring(z + e, 16), c)

    def tile_at(e):
        return {"tile": ring(t + e, 32), "chan": k}

    other = device(x, y, z, 1 - c)

    def send(src, dst, send_sem, recv_sem, to):
        pltpu.make_async_remote_copy(
            src_ref=src, dst_ref=dst, send_sem=send_sem, recv_sem=recv_sem,
            device_id=to, device_id_type=MESH,
        ).start()

    def await_bytes(view, sem):
        pltpu.make_async_copy(view, view, sem).wait()

    fetches = [
        pltpu.make_async_copy(src, dst, fetch_s.at[i])
        for i, (src, dst) in enumerate((
            (w_in_hbm, W.at[zh, y, zl, c, 0:TALL]), (w_out_hbm, W.at[zh, y, zl, c, TALL : 2 * TALL]), (f_hbm, f_ref),
            (table_hbm, table_ref), (dw_bias_hbm, dw_bias_ref), (b_out_hbm, b_out_ref),
            (gamma_hbm, gamma_ref), (gain_hbm, gain_ref), (shift_hbm, shift_ref),
            (b_in_hbm, b_in_ref),
        ))
    ]

    barrier = pltpu.get_barrier_semaphore()
    partners = [tile_at(1), tile_at(-1), x_at(1), x_at(2), x_at(3), y_at(1), y_at(2), y_at(-1)]
    partners += [z_at(1), z_at(-1), z_at(2), z_at(-2), z_at(6), z_at(-6), other]
    for partner in partners:
        pl.semaphore_signal(barrier, inc=1, device_id=partner, device_id_type=MESH)
    for fetch in fetches:
        fetch.start()

    def slot(yy, zz):
        return W.at[lax.div(zz, 4), yy, lax.rem(zz, 4), c, 0:HEAD]

    def bundle(zz):
        return W.at[lax.div(zz, 4), :, lax.rem(zz, 4), c, HEAD : 2 * TALL]

    def rest(yy):
        return W.at[zh, yy, zl, c, HEAD : 2 * TALL]

    for fetch in fetches:
        fetch.wait()
    pl.semaphore_wait(barrier, len(partners))

    send(f_ref.at[5:8], halo.at[0], halo_s.at[0], halo_r.at[0], tile_at(1))
    send(f_ref.at[0:3], halo.at[1], halo_s.at[1], halo_r.at[1], tile_at(-1))

    reach = {1: 8, -1: 7}

    def along(off):
        return [way for way in (1, -1) if off * way <= 0 and -off * way < reach[way]]

    def heading(off):
        return 1 if off <= 0 else -1

    def cross(o, piece):
        send(piece, piece, cs.at[o], cr.at[o], other)

    def spread(off):
        piece = slot(y, ring(z + off, 16))
        for way in along(off):
            i = (1 - way) // 2
            send(piece, piece, zs.at[i, -off * way], zr.at[i, -off * way], z_at(way))
        onward = heading(off)
        send(piece, piece, ys.at[0], yf.at[off % 16], y_at(onward))
        send(piece, piece, ys.at[1], yb.at[off % 16], y_at(-onward))
        cross(0, piece)

    def pass_on(off):
        onward = heading(off)
        piece = slot(ring(y - onward, 4), ring(z + off, 16))
        await_bytes(piece, yf.at[off % 16])
        send(piece, piece, ys.at[2], yq.at[off % 16], y_at(onward))
        cross(-onward % 4, piece)
        piece = slot(ring(y + onward, 4), ring(z + off, 16))
        await_bytes(piece, yb.at[off % 16])
        cross(onward % 4, piece)

    def last(off):
        piece = slot(ring(y + 2, 4), ring(z + off, 16))
        await_bytes(piece, yq.at[off % 16])
        cross(2, piece)

    def tick(s):
        for way in (1, -1):
            if s <= reach[way]:
                await_bytes(slot(y, ring(z - s * way, 16)), zr.at[(1 - way) // 2, s - 1])
                spread(-s * way)

    def relay(s, action):
        for way in (1, -1):
            if s == 0 and way == 1:
                action(0)
            if s > 0 and s <= reach[way]:
                action(-s * way)

    def pass_bundle(off):
        piece = bundle(ring(z + off, 16))
        for way in along(off):
            i = (1 - way) // 2
            send(piece, piece, ts.at[i], tr.at[i, -off * way], z_at(way))
        send(piece, piece, tc_s, tc_r, other)

    def tick_bundle(s):
        if s == 0:
            for e in (1, 2, 3):
                await_bytes(rest(ring(y - e, 4)), ty_r.at[e - 1])
            pass_bundle(0)
        for way in (1, -1):
            if 0 < s <= reach[way]:
                await_bytes(bundle(ring(z - s * way, 16)), tr.at[(1 - way) // 2, s - 1])
                pass_bundle(-s * way)

    spread(0)
    for e in (1, 3, 2):
        send(rest(y), rest(y), ty_s.at[e - 1], ty_r.at[e - 1], y_at(e))

    for j in range(3):
        own_b[:, 128 * j : 128 * j + 128] = jnp.broadcast_to(b_in_ref[j : j + 1, :], (8, 128))

    def step(s):
        if s <= 8:
            tick(s)
        if s <= 9:
            tick_bundle(s - 1)
            relay(s - 1, pass_on)
        if s >= 2:
            relay(s - 2, last)

    lane = lax.broadcasted_iota(jnp.int32, (1, 128), 1)
    columns[...] = table_ref[...].T

    def spread_table(i, carry):
        at = pl.ds(pl.multiple_of(i * 8, 8), 8)
        table = columns[at, :]
        for j in range(TAPS):
            d = j % 7 - 3
            value = jnp.broadcast_to(table[:, j : j + 1], (8, 128))
            if d != 0:
                inside = lane >= d if d > 0 else lane < 128 + d
                value = jnp.where(inside, value, 0.0)
            planes[j, at, :] = value
        diagonal = (
            lax.broadcasted_iota(jnp.int32, (8, SLAB), 0) + i * 8
            == lax.broadcasted_iota(jnp.int32, (8, SLAB), 1)
        )
        for j, ref in ((BIAS, dw_bias_ref), (OUT_BIAS, b_out_ref), (SCALE, gamma_ref)):
            column = jnp.sum(jnp.where(diagonal, ref[...], 0.0), axis=1, keepdims=True)
            planes[j, at, :] = jnp.broadcast_to(column, (8, 128))
        return carry

    lax.fori_loop(0, 12, spread_table, 0)

    def widen(i, carry):
        at = pl.ds(pl.multiple_of(i * 16, 16), 16)
        wide[:, at, :] = f_ref[:, at, :].astype(F32)
        return carry

    lax.fori_loop(0, 6, widen, 0)

    def taps(rows, at, pairs):
        total = [None] * len(pairs)
        for tap_col in range(7):
            d = tap_col - 3
            weight = {}
            for r, pair in enumerate(pairs):
                part = None
                for e, tap_row in pair:
                    if tap_row not in weight:
                        weight[tap_row] = planes[tap_row * 7 + tap_col, at, :]
                    product = rows[e] * weight[tap_row]
                    part = product if part is None else part + product
                if d != 0:
                    part = pltpu.roll(part, (-d) % 128, 1)
                total[r] = part if total[r] is None else total[r] + part
        return total

    def own_rows(i, carry):
        at = pl.ds(pl.multiple_of(i * 8, 8), 8)
        rows = [wide[r, at, :] for r in range(8)]
        pairs = [[(e, e - r + 3) for e in range(8) if 0 <= e - r + 3 < 7] for r in range(8)]
        bias = planes[BIAS, at, :]
        for r, part in enumerate(taps(rows, at, pairs)):
            conv[r, at, :] = part + bias
        return carry

    lax.fori_loop(0, 12, own_rows, 0)
    step(1)

    await_bytes(halo.at[0], halo_r.at[0])
    await_bytes(halo.at[1], halo_r.at[1])

    @pl.when(t == 0)
    def _():
        halo[0] = jnp.zeros((3, SLAB, 128), BF16)

    @pl.when(t == 31)
    def _():
        halo[1] = jnp.zeros((3, SLAB, 128), BF16)

    def rims(i, carry):
        at = pl.ds(pl.multiple_of(i * 16, 16), 16)
        for side, first in ((0, 0), (1, 5)):
            rows = [halo[side, r, at, :].astype(F32) for r in range(3)]
            if side == 0:
                pairs = [[(e, e - r) for e in range(r, 3)] for r in range(3)]
            else:
                pairs = [[(e, e - r + 6) for e in range(r + 1)] for r in range(3)]
            for r, part in enumerate(taps(rows, at, pairs)):
                cv[first + r, at, :] = (conv[first + r, at, :] + part).astype(BF16)
        for r in (3, 4):
            cv[r, at, :] = conv[r, at, :].astype(BF16)
        return carry

    lax.fori_loop(0, 6, rims, 0)

    def block(kk):
        return xg.at[:, pl.ds(pl.multiple_of(kk * SLAB, SLAB), SLAB), :]

    for r in (1, 2, 0, 3):
        rows = pl.ds(2 * ring(zh + r, 4), 2)
        send(cv.at[rows], block(k), za_s.at[r], za_r.at[r], z_at(2 + 4 * r - 16 * (r // 2)))
    for r in range(4):
        to = z_at(2 + 4 * r - 16 * (r // 2))
        send(own_b, bb.at[zh], b_s.at[r], b_r.at[r], to)

    unit = ring(z - 2, 16)
    place, line = lax.div(unit, 4), lax.rem(unit, 4)

    def source(r):
        return ring(place - r, 4)

    def share(r):
        kk = x * 4 + source(r)
        for e in (2, 1, 3):
            send(block(kk), block(kk), xa_s.at[e - 1, r], xa_r.at[e - 1, r], x_at(e))

    def arrived(r):
        await_bytes(block(x * 4 + source(r)), za_r.at[r])
        share(r)

    for s in range(2, 11):
        step(s)
        if s == FIRST:
            arrived(0)
            arrived(3)
        if s == SECOND:
            arrived(1)
            arrived(2)
    for r in range(4):
        for e in (1, 2, 3):
            await_bytes(block(ring(x - e, 4) * 4 + source(r)), xa_r.at[e - 1, r])

    def load(j):
        return xg[:, pl.ds(pl.multiple_of(j * SLAB, SLAB), SLAB), :].astype(F32)

    def fold(v):
        return jnp.sum(v.reshape(2, SLAB // 8, 8, 128), axis=1)

    zero = jnp.zeros((2, 8, 128), F32)
    total = lax.fori_loop(0, 16, lambda j, s: s + fold(load(j)), zero)
    mean = jnp.sum(total, axis=1, keepdims=True) / 1536.0

    def squares(j, s):
        centered = load(j) - mean
        return s + fold(centered * centered)

    total = lax.fori_loop(0, 16, squares, zero)
    scale = lax.rsqrt(jnp.sum(total, axis=1, keepdims=True) / 1536.0 + 1e-6)

    def normalize(j, carry):
        at = pl.ds(pl.multiple_of(j * 128, 128), 128)
        for r in range(2):
            v = (xg[r, at, :].astype(F32) - mean[r]) * scale[r]
            v = v.T * gain_ref[pl.ds(j, 1), :] + shift_ref[pl.ds(j, 1), :]
            xt[r * 128 : r * 128 + 128, at] = v.astype(BF16)
        return carry

    lax.fori_loop(0, 12, normalize, 0)

    def row(yy, cc):
        return W.at[:, yy, :, cc, 0:HEAD]

    for o in range(4):
        await_bytes(row(ring(y + o, 4), 1 - c), cr.at[o])
    await_bytes(W.at[:, :, :, 1 - c, HEAD : 2 * TALL], tc_r)
    for r in range(4):
        await_bytes(bb.at[source(r)], b_r.at[r])

    def expand(g, carry):
        pre = jnp.dot(
            xt[...], W[g, :, :, :, 0:TALL].reshape(1536, COLS), preferred_element_type=F32
        )
        hid[g] = gelu(pre + bb[g, 0:1, :]).T.astype(BF16)
        return carry

    lax.fori_loop(0, 4, expand, 0)

    order = ((1, 2), (0, 3))

    def project(h, o):
        to_x = ring(y + o, 4)
        part = jnp.zeros((2 * SLAB, 256), F32)
        for g in range(4):
            weights = jnp.concatenate(
                [
                    W[g, to_x, source(n), :, TALL : 2 * TALL].reshape(SLAB, COLS)
                    for n in order[h]
                ],
                axis=0,
            )
            part = part + jnp.dot(weights, hid[g], preferred_element_type=F32)
        part = part.astype(BF16)
        for i in range(2):
            for r in range(2):
                ob[to_x, h, i, r] = part[SLAB * i : SLAB * i + SLAB, 128 * r : 128 * r + 128]

        @pl.when(to_x != x)
        def _():
            send(
                ob.at[to_x, h], rb.at[x, h], rs_s.at[to_x, h], rs_r.at[x, h],
                device(to_x, y, z, c),
            )

    for h in range(2):
        for o in (0, 1, -1, 2):
            project(h, o)

    for h in range(2):
        for e in (1, 2, 3):
            await_bytes(rb.at[ring(x + e, 4), h], rs_r.at[ring(x + e, 4), h])
        for i in range(2):
            def reduce(j, carry):
                at = pl.ds(pl.multiple_of(j * 32, 32), 32)
                total = ob[x, h, i, :, at, :].astype(F32)
                for e in (1, 2, 3):
                    total = total + rb[ring(x + e, 4), h, i, :, at, :].astype(F32)
                pz[h, i, :, at, :] = total.astype(BF16)
                return carry

            lax.fori_loop(0, 3, reduce, 0)
            n = order[h][i]
            send(
                pz.at[h, i], fin.at[pl.ds(2 * place, 2)], fin_s.at[n], fin_r.at[n],
                device(x, y, source(n) * 4 + line, c),
            )
    for n in (0, 3, 1, 2):
        await_bytes(fin.at[pl.ds(2 * ring(zh + n, 4), 2)], fin_r.at[n])

    def finish(i, carry):
        at = pl.ds(pl.multiple_of(i * 16, 16), 16)
        projected = fin[:, at, :].astype(F32) + planes[OUT_BIAS, at, :]
        o_ref[:, at, :] = (wide[:, at, :] + planes[SCALE, at, :] * projected).astype(BF16)
        return carry

    lax.fori_loop(0, 6, finish, 0)

    await_bytes(f_ref.at[5:8], halo_s.at[0])
    await_bytes(f_ref.at[0:3], halo_s.at[1])
    for n in range(4):
        await_bytes(cv.at[0:2], za_s.at[n])
        await_bytes(own_b, b_s.at[n])
        for e in range(3):
            await_bytes(cv.at[0:2], xa_s.at[e, n])
        await_bytes(cv.at[0:2], fin_s.at[n])
        for h in range(2):
            if n > 0:
                await_bytes(ob.at[0, 0], rs_s.at[ring(x + n, 4), h])
    for way in (1, -1):
        i = (1 - way) // 2
        await_bytes(xt.at[0 : 16 * reach[way]], ts.at[i])
        for n in range(reach[way]):
            await_bytes(slot(y, z), zs.at[i, n])
    for e in range(3):
        await_bytes(rest(y), ty_s.at[e])
    await_bytes(W.at[:, :, :, c, HEAD : 2 * TALL], tc_s)
    for i in range(3):
        await_bytes(row(y, c), ys.at[i])
    for o in range(4):
        await_bytes(row(y, c), cs.at[o])


def local(features, dw_weight, dw_bias, ln_gain, ln_bias, w_in, b_in, w_out, b_out, gamma):
    dma = pltpu.SemaphoreType.DMA
    vmem = pl.BlockSpec(memory_space=pltpu.VMEM)
    return pl.pallas_call(
        body,
        out_shape=jax.ShapeDtypeStruct(features.shape, BF16),
        in_specs=[pl.BlockSpec(memory_space=pltpu.HBM)] * 10,
        out_specs=vmem,
        scratch_shapes=[
            pltpu.VMEM((8, SLAB, 128), BF16),
            pltpu.VMEM((TAPS, SLAB), F32),
            pltpu.VMEM((1, SLAB), F32),
            pltpu.VMEM((1, SLAB), F32),
            pltpu.VMEM((1, SLAB), F32),
            pltpu.VMEM((12, 128), F32),
            pltpu.VMEM((12, 128), F32),
            pltpu.VMEM((3, 128), F32),
            dma((10,)),
            pltpu.VMEM((SLAB, TAPS), F32),
            pltpu.VMEM((TAPS + 3, SLAB, 128), F32),
            pltpu.VMEM((8, SLAB, 128), F32),
            pltpu.VMEM((2, 3, SLAB, 128), BF16),
            pltpu.VMEM((8, SLAB, 128), F32),
            pltpu.VMEM((8, SLAB, 128), BF16),
            pltpu.VMEM((2, 1536, 128), BF16),
            pltpu.VMEM((256, 1536), BF16),
            pltpu.VMEM((4, COLS, 256), BF16),
            pltpu.VMEM((4, 2, 2, 2, SLAB, 128), BF16),
            pltpu.VMEM((4, 2, 2, 2, SLAB, 128), BF16),
            pltpu.VMEM((2, 2, 2, SLAB, 128), BF16),
            pltpu.VMEM((8, SLAB, 128), BF16),
            pltpu.VMEM((4, 4, 4, 2, 2 * TALL, COLS), BF16),
            pltpu.VMEM((8, COLS), F32),
            pltpu.VMEM((4, 8, COLS), F32),
            dma((2,)), dma((2,)),
            dma((4,)), dma((4,)),
            dma((4,)), dma((4,)),
            dma((3, 4)), dma((3, 4)),
            dma((4, 2)), dma((4, 2)),
            dma((4,)), dma((4,)),
            dma((2, 8)), dma((2, 8)),
            dma((3,)), dma((16,)), dma((16,)), dma((16,)),
            dma((4,)), dma((4,)),
            dma((3,)), dma((3,)), dma((2,)), dma((2, 8)), dma, dma,
        ],
        compiler_params=pltpu.CompilerParams(
            collective_id=0, has_side_effects=True, vmem_limit_bytes=62 * 2**20
        ),
        name="block",
    )(
        features, dw_weight.T, dw_bias[None, :], b_out[None, :], gamma[None, :],
        ln_gain.reshape(12, 128), ln_bias.reshape(12, 128), w_in, b_in.reshape(3, 128), w_out.T,
    )


def solution(mesh):
    placed = (
        P("tile", "chan", None),
        P("chan", None),
        P("chan"),
        P(),
        P(),
        P("tile", "chan"),
        P("chan"),
        P("chan", "tile"),
        P("chan"),
        P("chan"),
    )
    return jax.shard_map(
        local, mesh=mesh, in_specs=placed, out_specs=P("tile", "chan", None), check_vma=False
    )
```

```python
import functools

import jax
import jax.numpy as jnp
from jax import lax
from jax.experimental import pallas as pl
from jax.experimental.pallas import tpu as pltpu
from jax.sharding import PartitionSpec as P

MESH = pl.DeviceIdType.MESH
F32 = jnp.float32
BF16 = jnp.bfloat16

SLAB = 96
COLS = 384
TALL = 48
HEAD = 80
TAPS = 49
FIRST, SECOND = 7, 9
BIAS, OUT_BIAS, SCALE = 49, 50, 51

ERF_NUM = (
    0.00022905065861350646,
    0.0034082910107109506,
    0.050955695062380861,
    0.18520832239976145,
    1.128379143519084,
)
ERF_DEN = (
    -1.1791602954361697e-7,
    0.000023547966471313185,
    0.0010179625278914885,
    0.014070470171167667,
    0.11098505178285362,
    0.49746925110067538,
    1.0,
)


def poly(x, coefficients):
    total = jnp.full_like(x, coefficients[0])
    for coefficient in coefficients[1:]:
        total = total * x + coefficient
    return total


def gelu(v):
    u = jnp.clip(v * 0.7071067811865476, -3.832506856900711, 3.832506856900711)
    square = u * u
    erf = u * poly(square, ERF_NUM) / poly(square, ERF_DEN)
    return 0.5 * v * (1.0 + erf)


def body(
    f_hbm, table_hbm, dw_bias_hbm, b_out_hbm, gamma_hbm, gain_hbm, shift_hbm, w_in_hbm,
    b_in_hbm, w_out_hbm, o_ref,
    f_ref, table_ref, dw_bias_ref, b_out_ref, gamma_ref, gain_ref, shift_ref, b_in_ref,
    fetch_s, columns, planes, wide, halo, conv, cv, xg, xt, hid, ob, rb, pz, fin, W, own_b, bb,
    halo_s, halo_r, za_s, za_r, b_s, b_r, xa_s, xa_r, rs_s, rs_r, fin_s, fin_r,
    zs, zr, ys, yf, yb, yq, cs, cr, ty_s, ty_r, ts, tr, tc_s, tc_r,
):
    t = lax.axis_index("tile")
    k = lax.axis_index("chan")
    x, zh = lax.div(k, 4), lax.rem(k, 4)
    y, zl, c = lax.div(t, 8), lax.rem(lax.div(t, 2), 4), lax.rem(t, 2)
    z = zh * 4 + zl

    def device(xx, yy, zz, cc):
        return {
            "tile": (yy * 4 + lax.rem(zz, 4)) * 2 + cc,
            "chan": xx * 4 + lax.div(zz, 4),
        }

    def ring(value, size):
        return lax.rem(value + size, size)

    def x_at(e):
        return device(ring(x + e, 4), y, z, c)

    def y_at(e):
        return device(x, ring(y + e, 4), z, c)

    def z_at(e):
        return device(x, y, ring(z + e, 16), c)

    def tile_at(e):
        return {"tile": ring(t + e, 32), "chan": k}

    other = device(x, y, z, 1 - c)

    def send(src, dst, send_sem, recv_sem, to):
        pltpu.make_async_remote_copy(
            src_ref=src, dst_ref=dst, send_sem=send_sem, recv_sem=recv_sem,
            device_id=to, device_id_type=MESH,
        ).start()

    def await_bytes(view, sem):
        pltpu.make_async_copy(view, view, sem).wait()

    fetches = [
        pltpu.make_async_copy(src, dst, fetch_s.at[i])
        for i, (src, dst) in enumerate((
            (w_in_hbm, W.at[zh, y, zl, c, 0:TALL]), (w_out_hbm, W.at[zh, y, zl, c, TALL : 2 * TALL]), (f_hbm, f_ref),
            (table_hbm, table_ref), (dw_bias_hbm, dw_bias_ref), (b_out_hbm, b_out_ref),
            (gamma_hbm, gamma_ref), (gain_hbm, gain_ref), (shift_hbm, shift_ref),
            (b_in_hbm, b_in_ref),
        ))
    ]

    barrier = pltpu.get_barrier_semaphore()
    partners = [tile_at(1), tile_at(-1), x_at(1), x_at(2), x_at(3), y_at(1), y_at(2), y_at(-1)]
    partners += [z_at(1), z_at(-1), z_at(2), z_at(-2), z_at(6), z_at(-6), other]
    for partner in partners:
        pl.semaphore_signal(barrier, inc=1, device_id=partner, device_id_type=MESH)
    for fetch in fetches:
        fetch.start()

    def slot(yy, zz):
        return W.at[lax.div(zz, 4), yy, lax.rem(zz, 4), c, 0:HEAD]

    def bundle(zz):
        return W.at[lax.div(zz, 4), :, lax.rem(zz, 4), c, HEAD : 2 * TALL]

    def rest(yy):
        return W.at[zh, yy, zl, c, HEAD : 2 * TALL]

    for fetch in fetches:
        fetch.wait()
    pl.semaphore_wait(barrier, len(partners))

    send(f_ref.at[5:8], halo.at[0], halo_s.at[0], halo_r.at[0], tile_at(1))
    send(f_ref.at[0:3], halo.at[1], halo_s.at[1], halo_r.at[1], tile_at(-1))

    reach = {1: 8, -1: 7}

    def along(off):
        return [way for way in (1, -1) if off * way <= 0 and -off * way < reach[way]]

    def heading(off):
        return 1 if off <= 0 else -1

    def cross(o, piece):
        send(piece, piece, cs.at[o], cr.at[o], other)

    def spread(off):
        piece = slot(y, ring(z + off, 16))
        for way in along(off):
            i = (1 - way) // 2
            send(piece, piece, zs.at[i, -off * way], zr.at[i, -off * way], z_at(way))
        onward = heading(off)
        send(piece, piece, ys.at[0], yf.at[off % 16], y_at(onward))
        send(piece, piece, ys.at[1], yb.at[off % 16], y_at(-onward))
        cross(0, piece)

    def pass_on(off):
        onward = heading(off)
        piece = slot(ring(y - onward, 4), ring(z + off, 16))
        await_bytes(piece, yf.at[off % 16])
        send(piece, piece, ys.at[2], yq.at[off % 16], y_at(onward))
        cross(-onward % 4, piece)
        piece = slot(ring(y + onward, 4), ring(z + off, 16))
        await_bytes(piece, yb.at[off % 16])
        cross(onward % 4, piece)

    def last(off):
        piece = slot(ring(y + 2, 4), ring(z + off, 16))
        await_bytes(piece, yq.at[off % 16])
        cross(2, piece)

    def tick(s):
        for way in (1, -1):
            if s <= reach[way]:
                await_bytes(slot(y, ring(z - s * way, 16)), zr.at[(1 - way) // 2, s - 1])
                spread(-s * way)

    def relay(s, action):
        for way in (1, -1):
            if s == 0 and way == 1:
                action(0)
            if s > 0 and s <= reach[way]:
                action(-s * way)

    def pass_bundle(off):
        piece = bundle(ring(z + off, 16))
        for way in along(off):
            i = (1 - way) // 2
            send(piece, piece, ts.at[i], tr.at[i, -off * way], z_at(way))
        send(piece, piece, tc_s, tc_r, other)

    def tick_bundle(s):
        if s == 0:
            for e in (1, 2, 3):
                await_bytes(rest(ring(y - e, 4)), ty_r.at[e - 1])
            pass_bundle(0)
        for way in (1, -1):
            if 0 < s <= reach[way]:
                await_bytes(bundle(ring(z - s * way, 16)), tr.at[(1 - way) // 2, s - 1])
                pass_bundle(-s * way)

    spread(0)
    for e in (1, 3, 2):
        send(rest(y), rest(y), ty_s.at[e - 1], ty_r.at[e - 1], y_at(e))

    for j in range(3):
        own_b[:, 128 * j : 128 * j + 128] = jnp.broadcast_to(b_in_ref[j : j + 1, :], (8, 128))

    def step(s):
        if s <= 8:
            tick(s)
        if s <= 9:
            relay(s - 1, pass_on)
        if s >= 2:
            relay(s - 2, last)
        if s <= 9:
            tick_bundle(s - 1)

    lane = lax.broadcasted_iota(jnp.int32, (1, 128), 1)
    columns[...] = table_ref[...].T

    def spread_table(i, carry):
        at = pl.ds(pl.multiple_of(i * 8, 8), 8)
        table = columns[at, :]
        for j in range(TAPS):
            d = j % 7 - 3
            value = jnp.broadcast_to(table[:, j : j + 1], (8, 128))
            if d != 0:
                inside = lane >= d if d > 0 else lane < 128 + d
                value = jnp.where(inside, value, 0.0)
            planes[j, at, :] = value
        diagonal = (
            lax.broadcasted_iota(jnp.int32, (8, SLAB), 0) + i * 8
            == lax.broadcasted_iota(jnp.int32, (8, SLAB), 1)
        )
        for j, ref in ((BIAS, dw_bias_ref), (OUT_BIAS, b_out_ref), (SCALE, gamma_ref)):
            column = jnp.sum(jnp.where(diagonal, ref[...], 0.0), axis=1, keepdims=True)
            planes[j, at, :] = jnp.broadcast_to(column, (8, 128))
        return carry

    lax.fori_loop(0, 12, spread_table, 0)

    def widen(i, carry):
        at = pl.ds(pl.multiple_of(i * 16, 16), 16)
        wide[:, at, :] = f_ref[:, at, :].astype(F32)
        return carry

    lax.fori_loop(0, 6, widen, 0)

    def taps(rows, at, pairs):
        total = [None] * len(pairs)
        for tap_col in range(7):
            d = tap_col - 3
            weight = {}
            for r, pair in enumerate(pairs):
                part = None
                for e, tap_row in pair:
                    if tap_row not in weight:
                        weight[tap_row] = planes[tap_row * 7 + tap_col, at, :]
                    product = rows[e] * weight[tap_row]
                    part = product if part is None else part + product
                if d != 0:
                    part = pltpu.roll(part, (-d) % 128, 1)
                total[r] = part if total[r] is None else total[r] + part
        return total

    def own_rows(i, carry):
        at = pl.ds(pl.multiple_of(i * 8, 8), 8)
        rows = [wide[r, at, :] for r in range(8)]
        pairs = [[(e, e - r + 3) for e in range(8) if 0 <= e - r + 3 < 7] for r in range(8)]
        bias = planes[BIAS, at, :]
        for r, part in enumerate(taps(rows, at, pairs)):
            conv[r, at, :] = part + bias
        return carry

    lax.fori_loop(0, 12, own_rows, 0)
    step(1)

    await_bytes(halo.at[0], halo_r.at[0])
    await_bytes(halo.at[1], halo_r.at[1])

    @pl.when(t == 0)
    def _():
        halo[0] = jnp.zeros((3, SLAB, 128), BF16)

    @pl.when(t == 31)
    def _():
        halo[1] = jnp.zeros((3, SLAB, 128), BF16)

    def rims(i, carry):
        at = pl.ds(pl.multiple_of(i * 16, 16), 16)
        for side, first in ((0, 0), (1, 5)):
            rows = [halo[side, r, at, :].astype(F32) for r in range(3)]
            if side == 0:
                pairs = [[(e, e - r) for e in range(r, 3)] for r in range(3)]
            else:
                pairs = [[(e, e - r + 6) for e in range(r + 1)] for r in range(3)]
            for r, part in enumerate(taps(rows, at, pairs)):
                cv[first + r, at, :] = (conv[first + r, at, :] + part).astype(BF16)
        for r in (3, 4):
            cv[r, at, :] = conv[r, at, :].astype(BF16)
        return carry

    lax.fori_loop(0, 6, rims, 0)

    def block(kk):
        return xg.at[:, pl.ds(pl.multiple_of(kk * SLAB, SLAB), SLAB), :]

    for r in (1, 2, 0, 3):
        rows = pl.ds(2 * ring(zh + r, 4), 2)
        send(cv.at[rows], block(k), za_s.at[r], za_r.at[r], z_at(2 + 4 * r - 16 * (r // 2)))
    for r in range(4):
        to = z_at(2 + 4 * r - 16 * (r // 2))
        send(own_b, bb.at[zh], b_s.at[r], b_r.at[r], to)

    unit = ring(z - 2, 16)
    place, line = lax.div(unit, 4), lax.rem(unit, 4)

    def source(r):
        return ring(place - r, 4)

    def share(r):
        kk = x * 4 + source(r)
        for e in (2, 1, 3):
            send(block(kk), block(kk), xa_s.at[e - 1, r], xa_r.at[e - 1, r], x_at(e))

    def arrived(r):
        await_bytes(block(x * 4 + source(r)), za_r.at[r])
        share(r)

    for s in range(2, 11):
        step(s)
        if s == FIRST:
            arrived(0)
            arrived(3)
        if s == SECOND:
            arrived(1)
            arrived(2)
    for r in range(4):
        for e in (1, 2, 3):
            await_bytes(block(ring(x - e, 4) * 4 + source(r)), xa_r.at[e - 1, r])

    def load(j):
        return xg[:, pl.ds(pl.multiple_of(j * SLAB, SLAB), SLAB), :].astype(F32)

    def fold(v):
        return jnp.sum(v.reshape(2, SLAB // 8, 8, 128), axis=1)

    zero = jnp.zeros((2, 8, 128), F32)
    total = lax.fori_loop(0, 16, lambda j, s: s + fold(load(j)), zero)
    mean = jnp.sum(total, axis=1, keepdims=True) / 1536.0

    def squares(j, s):
        centered = load(j) - mean
        return s + fold(centered * centered)

    total = lax.fori_loop(0, 16, squares, zero)
    scale = lax.rsqrt(jnp.sum(total, axis=1, keepdims=True) / 1536.0 + 1e-6)

    def normalize(j, carry):
        at = pl.ds(pl.multiple_of(j * 128, 128), 128)
        for r in range(2):
            v = (xg[r, at, :].astype(F32) - mean[r]) * scale[r]
            v = v.T * gain_ref[pl.ds(j, 1), :] + shift_ref[pl.ds(j, 1), :]
            xt[r * 128 : r * 128 + 128, at] = v.astype(BF16)
        return carry

    lax.fori_loop(0, 12, normalize, 0)

    def row(yy, cc):
        return W.at[:, yy, :, cc, 0:HEAD]

    for o in range(4):
        await_bytes(row(ring(y + o, 4), 1 - c), cr.at[o])
    await_bytes(W.at[:, :, :, 1 - c, HEAD : 2 * TALL], tc_r)
    for r in range(4):
        await_bytes(bb.at[source(r)], b_r.at[r])

    def expand(g, carry):
        pre = jnp.dot(
            xt[...], W[g, :, :, :, 0:TALL].reshape(1536, COLS), preferred_element_type=F32
        )
        hid[g] = gelu(pre + bb[g, 0:1, :]).T.astype(BF16)
        return carry

    lax.fori_loop(0, 4, expand, 0)

    order = ((1, 2), (0, 3))

    def project(h, o):
        to_x = ring(y + o, 4)
        part = jnp.zeros((2 * SLAB, 256), F32)
        for g in range(4):
            weights = jnp.concatenate(
                [
                    W[g, to_x, source(n), :, TALL : 2 * TALL].reshape(SLAB, COLS)
                    for n in order[h]
                ],
                axis=0,
            )
            part = part + jnp.dot(weights, hid[g], preferred_element_type=F32)
        part = part.astype(BF16)
        for i in range(2):
            for r in range(2):
                ob[to_x, h, i, r] = part[SLAB * i : SLAB * i + SLAB, 128 * r : 128 * r + 128]

        @pl.when(to_x != x)
        def _():
            send(
                ob.at[to_x, h], rb.at[x, h], rs_s.at[to_x, h], rs_r.at[x, h],
                device(to_x, y, z, c),
            )

    for h in range(2):
        for o in (0, 1, -1, 2):
            project(h, o)

    for h in range(2):
        for e in (1, 2, 3):
            await_bytes(rb.at[ring(x + e, 4), h], rs_r.at[ring(x + e, 4), h])
        for i in range(2):
            def reduce(j, carry):
                at = pl.ds(pl.multiple_of(j * 32, 32), 32)
                total = ob[x, h, i, :, at, :].astype(F32)
                for e in (1, 2, 3):
                    total = total + rb[ring(x + e, 4), h, i, :, at, :].astype(F32)
                pz[h, i, :, at, :] = total.astype(BF16)
                return carry

            lax.fori_loop(0, 3, reduce, 0)
            n = order[h][i]
            send(
                pz.at[h, i], fin.at[pl.ds(2 * place, 2)], fin_s.at[n], fin_r.at[n],
                device(x, y, source(n) * 4 + line, c),
            )
    for n in (0, 3, 1, 2):
        await_bytes(fin.at[pl.ds(2 * ring(zh + n, 4), 2)], fin_r.at[n])

    def finish(i, carry):
        at = pl.ds(pl.multiple_of(i * 16, 16), 16)
        projected = fin[:, at, :].astype(F32) + planes[OUT_BIAS, at, :]
        o_ref[:, at, :] = (wide[:, at, :] + planes[SCALE, at, :] * projected).astype(BF16)
        return carry

    lax.fori_loop(0, 6, finish, 0)

    await_bytes(f_ref.at[5:8], halo_s.at[0])
    await_bytes(f_ref.at[0:3], halo_s.at[1])
    for n in range(4):
        await_bytes(cv.at[0:2], za_s.at[n])
        await_bytes(own_b, b_s.at[n])
        for e in range(3):
            await_bytes(cv.at[0:2], xa_s.at[e, n])
        await_bytes(cv.at[0:2], fin_s.at[n])
        for h in range(2):
            if n > 0:
                await_bytes(ob.at[0, 0], rs_s.at[ring(x + n, 4), h])
    for way in (1, -1):
        i = (1 - way) // 2
        await_bytes(xt.at[0 : 16 * reach[way]], ts.at[i])
        for n in range(reach[way]):
            await_bytes(slot(y, z), zs.at[i, n])
    for e in range(3):
        await_bytes(rest(y), ty_s.at[e])
    await_bytes(W.at[:, :, :, c, HEAD : 2 * TALL], tc_s)
    for i in range(3):
        await_bytes(row(y, c), ys.at[i])
    for o in range(4):
        await_bytes(row(y, c), cs.at[o])


def local(features, dw_weight, dw_bias, ln_gain, ln_bias, w_in, b_in, w_out, b_out, gamma):
    dma = pltpu.SemaphoreType.DMA
    vmem = pl.BlockSpec(memory_space=pltpu.VMEM)
    return pl.pallas_call(
        body,
        out_shape=jax.ShapeDtypeStruct(features.shape, BF16),
        in_specs=[pl.BlockSpec(memory_space=pltpu.HBM)] * 10,
        out_specs=vmem,
        scratch_shapes=[
            pltpu.VMEM((8, SLAB, 128), BF16),
            pltpu.VMEM((TAPS, SLAB), F32),
            pltpu.VMEM((1, SLAB), F32),
            pltpu.VMEM((1, SLAB), F32),
            pltpu.VMEM((1, SLAB), F32),
            pltpu.VMEM((12, 128), F32),
            pltpu.VMEM((12, 128), F32),
            pltpu.VMEM((3, 128), F32),
            dma((10,)),
            pltpu.VMEM((SLAB, TAPS), F32),
            pltpu.VMEM((TAPS + 3, SLAB, 128), F32),
            pltpu.VMEM((8, SLAB, 128), F32),
            pltpu.VMEM((2, 3, SLAB, 128), BF16),
            pltpu.VMEM((8, SLAB, 128), F32),
            pltpu.VMEM((8, SLAB, 128), BF16),
            pltpu.VMEM((2, 1536, 128), BF16),
            pltpu.VMEM((256, 1536), BF16),
            pltpu.VMEM((4, COLS, 256), BF16),
            pltpu.VMEM((4, 2, 2, 2, SLAB, 128), BF16),
            pltpu.VMEM((4, 2, 2, 2, SLAB, 128), BF16),
            pltpu.VMEM((2, 2, 2, SLAB, 128), BF16),
            pltpu.VMEM((8, SLAB, 128), BF16),
            pltpu.VMEM((4, 4, 4, 2, 2 * TALL, COLS), BF16),
            pltpu.VMEM((8, COLS), F32),
            pltpu.VMEM((4, 8, COLS), F32),
            dma((2,)), dma((2,)),
            dma((4,)), dma((4,)),
            dma((4,)), dma((4,)),
            dma((3, 4)), dma((3, 4)),
            dma((4, 2)), dma((4, 2)),
            dma((4,)), dma((4,)),
            dma((2, 8)), dma((2, 8)),
            dma((3,)), dma((16,)), dma((16,)), dma((16,)),
            dma((4,)), dma((4,)),
            dma((3,)), dma((3,)), dma((2,)), dma((2, 8)), dma, dma,
        ],
        compiler_params=pltpu.CompilerParams(
            collective_id=0, has_side_effects=True, vmem_limit_bytes=62 * 2**20
        ),
        name="block",
    )(
        features, dw_weight.T, dw_bias[None, :], b_out[None, :], gamma[None, :],
        ln_gain.reshape(12, 128), ln_bias.reshape(12, 128), w_in, b_in.reshape(3, 128), w_out.T,
    )


def solution(mesh):
    placed = (
        P("tile", "chan", None),
        P("chan", None),
        P("chan"),
        P(),
        P(),
        P("tile", "chan"),
        P("chan"),
        P("chan", "tile"),
        P("chan"),
        P("chan"),
    )
    return jax.shard_map(
        local, mesh=mesh, in_specs=placed, out_specs=P("tile", "chan", None), check_vma=False
    )
```
